32 devices in a mesh: groups: 2 (over x), tile: 16 (over z, y, core).
Axes of the slice: x: 2, y: 2, z: 4, core: 2. Of those that a mesh axis runs over, the one named last changes fastest.
Arguments:
- exposures: float32 [32, 8, 256, 256], P(('groups', 'tile')), parts along dimension 0, may hold values from -2400 to 2400
- row_taps: bfloat16 [5, 21], replicated, may hold values from -1.25 to 1.25
- col_taps: bfloat16 [5, 21], replicated, may hold values from -1.25 to 1.25
- kernel_coeffs: float32 [32, 8, 25, 6], P(('groups', 'tile')), parts along dimension 0, may hold values from -1.25 to 1.25
- subpixel: float32 [32, 8, 2], P(('groups', 'tile')), parts along dimension 0, may hold values from 0.1 to 0.9
- destination: int32 [32, 32], P('groups'), parts along dimension 0, may hold values from 0 to 63, as said below
Outputs:
- significance: float32 [32, 8, 4, 128, 128], P(('groups', 'tile')), parts along dimension 0
The draws below stay inside these ranges and needn't reach their ends.
There are 2 independent parts, one for each index of `groups`. The reference program is written for one: setup_inputs(seed, part) draws one part's arguments, and reference() takes and returns one part's arrays. A program takes and returns all parts, laid end to end along the dimension named above; an argument that names none is the same for every part. Nothing has to cross between parts.
Inputs may be any that keep to these rules, and one draw needn't show every extreme that they name: `destination`: entry [t, v * 4 + i] is the sky slot of block i of visit v of tile t; the slots o * 4 to (o + 1) * 4 - 1 are the patches of tile index o. Of the blocks of the 1 tiles of one tile index, at most 2 name slots of one tile index, and in every draw some tile index receives exactly 2 blocks from every tile index.
All inputs are finite; a program needn't handle non-finite values.
Results may differ from the reference program's by a relative error of at most 0.0062.
Values sent between devices are 32-bit elements; how exact they have to be, the bound alone decides.
No kernel may reach another device: no remote copies, remote signals or barrier semaphores. Data moves between devices by JAX's collectives and lax.ppermute only.
A program may use at most 128 MiB of HBM per device.

```python
import math
import jax
import jax.numpy as jnp
from jax import lax

TILE_DEV = 1
VISITS = 8
PIX = 256
BLOCK = 128
FILTERS = 5
TAPS = 21
NPOLY = 6
NB = 4
TILES = 16
CAP = 2


def draw_exposures(key, part):
    key_noise, key_visit, key_cols = jax.random.split(key, 3)
    place = jnp.arange(TILES, dtype=jnp.float32) / (TILES - 1)
    visit_gain = jnp.exp(jax.random.uniform(key_visit, (VISITS,), minval=0.0, maxval=math.log(4.0)))
    column_gain = jnp.exp(jax.random.uniform(key_cols, (PIX,), minval=0.0, maxval=math.log(10.0)))
    full_shape = (TILES, VISITS, PIX, PIX)
    noise = jax.random.truncated_normal(key_noise, -6.0, 6.0, full_shape)
    tile_gain = 10.0 ** place
    scaled = noise * tile_gain[:, None, None, None] * visit_gain[None, :, None, None]
    return (scaled * column_gain[None, None, None, :]).astype(jnp.float32)


def draw_destination(key, part):
    per_dev = TILE_DEV * VISITS * NB
    owners = TILES // TILE_DEV
    owned = TILE_DEV * NB
    key_heavy, key_order, key_slot = jax.random.split(jax.random.fold_in(key, 17), 3)
    heavy = jax.random.randint(key_heavy, (), 0, owners).astype(jnp.int32)
    spare = (owners - 1) * CAP
    tokens = (jnp.arange(spare, dtype=jnp.int32) // CAP).astype(jnp.int32)

    def one_device(device_key):
        key_rank, key_fill = jax.random.split(device_key)
        ranking = jax.random.permutation(key_rank, per_dev)
        chosen = jax.random.permutation(key_fill, spare)[:per_dev - CAP]
        others = tokens[chosen]
        others = others + (others >= heavy).astype(jnp.int32)
        listing = jnp.concatenate([jnp.zeros((CAP,), jnp.int32) + heavy, others.astype(jnp.int32)])
        return listing[ranking]
    owner_of = jax.vmap(one_device)(jax.random.split(key_order, owners))
    slot_in = jax.random.randint(key_slot, (owners, per_dev), 0, owned).astype(jnp.int32)
    return (owner_of * owned + slot_in).reshape(TILES, VISITS * NB).astype(jnp.int32)


def block_levels(key, dims, cuts, low, top_value):
    def one(axis_at, blocks):
        steps = jax.random.uniform(jax.random.fold_in(jax.random.fold_in(key, 6), axis_at), (blocks,), jnp.float32, low / len(cuts), top_value / len(cuts))
        return jnp.repeat(jnp.exp(steps), dims[axis_at] // blocks).reshape((-1,) + (1,) * (len(dims) - axis_at - 1))

    factor_of = one(*cuts[0])
    for cut in cuts[1:]:
        factor_of = factor_of * one(*cut)
    return factor_of


def bell_draw(stream_key, dims, deviation, reach, cuts=(), kind=jnp.bfloat16):
    drawn = jax.random.normal(stream_key, dims, jnp.float32) * deviation
    if len(cuts) > 0:
        drawn = block_levels(stream_key, dims, cuts, -0.22, 0.18) * drawn
    return jnp.clip(drawn, min=-reach, max=reach).astype(kind)


def setup_inputs(seed: int = 0, part: int = 0) -> dict:
    seeds = jax.random.split(jax.random.key(seed), 7)
    part_keys = jax.random.split(jax.random.fold_in(seeds[6], part), 7)
    return {
        "exposures": draw_exposures(jax.random.fold_in(jax.random.fold_in(seeds[6], part), 71), part),
        "row_taps": bell_draw(seeds[1], (FILTERS, TAPS), TAPS ** -0.5, 1.25),
        "col_taps": bell_draw(seeds[2], (FILTERS, TAPS), TAPS ** -0.5, 1.25),
        "kernel_coeffs": bell_draw(part_keys[3], (TILES, VISITS, FILTERS * FILTERS, NPOLY), (FILTERS * FILTERS) ** -0.5, 1.25, ((0, 16),), jnp.float32),
        "subpixel": jnp.clip(0.1 + 0.79999997 * jax.random.uniform(part_keys[4], (TILES, VISITS, 2), jnp.float32) ** block_levels(part_keys[4], (TILES, VISITS, 2), ((0, 16),), -0.2, 0.2), 0.1, 0.9),
        "destination": draw_destination(jax.random.fold_in(jax.random.fold_in(seeds[6], part), 71), part),
    }


highest = lax.Precision.HIGHEST

def banded(filter_taps, length):
    tap_count = filter_taps.shape[1]
    middle = tap_count // 2
    pixels = jnp.arange(length, dtype=jnp.int32)
    offset = pixels[None, :] - pixels[:, None] + middle
    selector = (offset[:, :, None] == jnp.arange(tap_count, dtype=jnp.int32)[None, None, :]).astype(jnp.float32)
    matrix = jnp.einsum('pqk,fk->fpq', selector, filter_taps.astype(jnp.float32), precision=highest)
    return matrix.astype(jnp.bfloat16)

def monomials(length):
    coordinate = 2.0 * jnp.arange(length, dtype=jnp.float32) / (length - 1) - 1.0
    unity = jnp.ones((length, length), jnp.float32)
    along_rows = coordinate[:, None] * unity
    along_cols = coordinate[None, :] * unity
    return jnp.stack([unity, along_rows, along_cols, along_rows * along_rows, along_rows * along_cols, along_cols * along_cols])

def match_one(picture, coeffs, row_stack, col_stack, mono_maps):
    length = picture.shape[0]
    filters = col_stack.shape[0] // length
    smooth = jnp.dot(picture.astype(jnp.bfloat16), row_stack, preferred_element_type=jnp.float32).astype(jnp.bfloat16)
    basis_maps = jnp.dot(col_stack, smooth, preferred_element_type=jnp.float32)
    basis_maps = basis_maps.reshape(filters, length, filters, length)
    poly_maps = jnp.einsum('aybx,abj->jyx', basis_maps, coeffs.reshape(filters, filters, -1), precision=highest)
    return lax.optimization_barrier(jnp.sum(mono_maps * poly_maps, axis=0))

def lanczos_matrix(offset_px, block_side):
    pixels = jnp.arange(block_side, dtype=jnp.float32)
    distance = pixels[:, None] - pixels[None, :] + offset_px[..., None, None]
    kernel = jnp.sinc(distance) * jnp.sinc(distance / 3.0)
    return jnp.where(jnp.abs(distance) < 3.0, kernel, 0.0)

def warp_blocks(blocks, shifts):
    block_side = blocks.shape[-1]
    vertical = lanczos_matrix(shifts[..., 0], block_side)
    horizontal = lanczos_matrix(shifts[..., 1], block_side)
    partial_value = jnp.einsum('...ji,...ik->...jk', vertical, blocks, precision=highest)
    return jnp.einsum('...jk,...lk->...jl', partial_value, horizontal, precision=highest)

def reference(exposures, row_taps, col_taps, kernel_coeffs, subpixel, destination):
    tile_total, visits, length = (exposures.shape[0], exposures.shape[1], exposures.shape[2])
    filters = row_taps.shape[0]
    block_side = BLOCK
    per_side = length // block_side
    block_count = per_side * per_side
    row_stack = jnp.transpose(banded(row_taps, length), (2, 0, 1)).reshape(length, filters * length)
    col_stack = banded(col_taps, length).reshape(filters * length, length)
    mono_maps = monomials(length)
    images = exposures.reshape(tile_total * visits, length, length)
    coeffs = kernel_coeffs.reshape(tile_total * visits, filters * filters, -1)
    matched = lax.map(lambda packed: match_one(packed[0], packed[1], row_stack, col_stack, mono_maps), (images, coeffs))
    power_sum = lax.optimization_barrier(jnp.sum((matched * matched).reshape(tile_total, visits, -1), axis=(0, 2)))
    variance = power_sum / (tile_total * length * length) + 1e-05
    blocks = matched.reshape(tile_total * visits, per_side, block_side, per_side, block_side)
    blocks = blocks.transpose(0, 1, 3, 2, 4).reshape(-1, block_side, block_side)
    shifts = jnp.repeat(subpixel.reshape(tile_total * visits, 2), block_count, axis=0)
    warped = warp_blocks(blocks, shifts)
    slot_of = destination.reshape(-1).astype(jnp.int32)
    visit_of = jnp.arange(slot_of.shape[0], dtype=jnp.int32) // block_count % visits
    weight = 1.0 / variance[visit_of]
    slot_total = tile_total * block_count
    numerator = jax.ops.segment_sum(warped * weight[:, None, None], slot_of, num_segments=slot_total)
    denominator = jax.ops.segment_sum(weight, slot_of, num_segments=slot_total)
    template = numerator / jnp.where(denominator > 0, denominator, 1.0)[:, None, None]
    significance = (warped - template[slot_of]) / jnp.sqrt(variance[visit_of])[:, None, None]
    return significance.reshape(tile_total, visits, block_count, block_side, block_side)
```

```python
import functools
import jax
import jax.numpy as jnp
from jax import lax
from jax.experimental import pallas as pl
from jax.experimental.pallas import tpu as pltpu
from jax.sharding import PartitionSpec as P

BLOCK = 128
LANES = 128
SEG = 32


def skew(rows8, base):
    base = base % LANES
    if base > LANES - 8:
        rows8 = pltpu.roll(rows8, 8, 1)
        base -= 8
    return pltpu.roll(rows8, base, 1, stride=1, stride_axis=0)


def iotas(rows):
    lane = lax.broadcasted_iota(jnp.int32, (rows, LANES), 1)
    row = lax.broadcasted_iota(jnp.int32, (rows, LANES), 0)
    return lane, lane - row


def split(x):
    high = x.astype(jnp.bfloat16)
    low = (x - high.astype(jnp.float32)).astype(jnp.bfloat16)
    return high, low


def banded_rows(tap_row, length, taps, first):
    lane, diff = iotas(8)
    wide = jnp.broadcast_to(tap_row, (8, LANES))
    tiles = []
    for start in range(0, length, 8):
        rolled = skew(wide, start + first)
        cols = []
        for tile in range(length // LANES):
            k = diff + (LANES * tile - start - first)
            cols.append(jnp.where((k >= 0) & (k < taps), rolled, 0.0))
        tiles.append(jnp.concatenate(cols, axis=1) if len(cols) > 1 else cols[0])
    return jnp.concatenate(tiles, axis=0)


def match_kernel(own_ref, x_ref, d_ref, taps_ref, warp_ref, *refs, filters, taps, strips, visits):
    outs = refs[:strips]
    rbig, s_win, h_win, powers, held = refs[strips:]
    step = pl.program_id(0)
    length = x_ref.shape[1]
    half = length // 2
    middle = taps // 2
    window = s_win.shape[2]
    win = -(-(half + middle) // 16) * 16

    @pl.when(step == 0)
    def _():
        for b in range(filters):
            band = banded_rows(taps_ref[b : b + 1, :], length, taps, -middle)
            rbig[:, b * length : (b + 1) * length] = band.astype(jnp.bfloat16)
        s_win[...] = jnp.zeros(s_win.shape, jnp.bfloat16)
        h_win[...] = jnp.zeros(h_win.shape, jnp.bfloat16)
        powers[...] = jnp.zeros(powers.shape, jnp.float32)

    image = x_ref[0].astype(jnp.bfloat16)
    for b in range(filters):
        smooth = jnp.dot(
            image, rbig[:, b * length : (b + 1) * length], preferred_element_type=jnp.float32
        ).astype(jnp.bfloat16)
        s_win[0, b * win : (b + 1) * win, :] = smooth[0:win]
        s_win[1, b * win : (b + 1) * win, :] = smooth[length - win :]

    lane, diff = iotas(8)
    for side in range(2):
        origin = side * (length - win)
        for group in range(half // 16):
            halves = []
            for sub in range(2):
                start = 16 * group + 8 * sub
                row = lax.broadcasted_iota(jnp.int32, (8, LANES), 0) + (side * half + start)
                u = 2.0 * row.astype(jnp.float32) / (length - 1) - 1.0
                compact = []
                for tile in range(d_ref.shape[2] // LANES):
                    sl = slice(tile * LANES, (tile + 1) * LANES)
                    compact.append(
                        d_ref[0, 0:1, sl] + u * (d_ref[0, 1:2, sl] + u * d_ref[0, 2:3, sl])
                    )
                acc = {}
                for b in range(filters):
                    lead = b * win + side * half + start - middle - origin
                    first = max(lead, b * win)
                    last = min(lead + 7 + taps - 1, (b + 1) * win - 1)
                    masks = {}
                    for tile in range(first // LANES, last // LANES + 1):
                        k = diff + (LANES * tile - lead)
                        mask = (k >= 0) & (k < taps)
                        if lead < b * win:
                            mask &= lane >= b * win - LANES * tile
                        if lead + 7 + taps > (b + 1) * win:
                            mask &= lane < (b + 1) * win - LANES * tile
                        masks[tile] = mask
                    for q in range(3):
                        seg = b * 3 + q
                        off = SEG * (seg % (LANES // SEG))
                        rolled = skew(compact[seg * SEG // LANES], lead - off)
                        for tile, mask in masks.items():
                            acc[q, tile] = jnp.where(mask, rolled, acc.get((q, tile), 0.0))
                halves.append(acc)
            for q, tile in sorted(set(halves[0]) | set(halves[1])):
                zero = jnp.zeros((8, LANES), jnp.float32)
                both = jnp.concatenate([h.get((q, tile), zero) for h in halves], axis=0)
                h_win[
                    side,
                    q * half + 16 * group : q * half + 16 * group + 16,
                    tile * LANES : (tile + 1) * LANES,
                ] = both.astype(jnp.bfloat16)

    col = lax.broadcasted_iota(jnp.int32, (1, length), 1).astype(jnp.float32)
    w = 2.0 * col / (length - 1) - 1.0
    vertical = split(banded_rows(warp_ref[0, 0:1, :], half, 6, -2))
    horizontal = split(banded_rows(warp_ref[0, 1:2, :], half, 6, -3))
    left = jnp.concatenate([vertical[0], vertical[0], vertical[1]], axis=1)
    right = jnp.concatenate([horizontal[0], horizontal[0], horizontal[1]], axis=0)
    power = jnp.zeros((1, LANES), jnp.float32)
    height = half // strips
    for side in range(2):
        z = jnp.dot(h_win[side], s_win[side], preferred_element_type=jnp.float32)
        matched = z[0:half] + w * (z[half : 2 * half] + w * z[2 * half :])
        squares = jnp.sum(matched * matched, axis=0, keepdims=True)
        power += squares[:, :half] + squares[:, half:]
        high, low = split(matched)
        stacked = jnp.concatenate([high, low, high], axis=0)
        moved = jnp.dot(left, stacked, preferred_element_type=jnp.float32)
        for c in range(2):
            high, low = split(moved[:, c * half : (c + 1) * half])
            lhs = jnp.concatenate([high, low, high], axis=1)
            warped = jnp.dot(lhs, right, preferred_element_type=jnp.float32)
            held[2 * side + c] = warped
    visit = pl.ds(step % visits, 1)
    powers[visit, :] = powers[visit, :] + power
    for k in range(strips):
        rows = pl.ds(pl.multiple_of(height * (own_ref[0] ^ k), height), height)
        for block in range(4):
            at = pl.ds(pl.multiple_of((4 * step + block) * height, height), height)
            outs[k][at, :] = held[block, rows, :]

    @pl.when(step == pl.num_programs(0) - 1)
    def _():
        for k in range(strips):
            outs[k][outs[k].shape[0] - powers.shape[0] :, :] = powers[...]


def match_and_warp(own, images, dtab, taps_rev, warp_taps, filters, taps, strips, visits):
    count, length, _ = images.shape
    half = length // 2
    win = -(-(half + taps // 2) // 16) * 16
    depth = -(-filters * win // LANES) * LANES
    pow_rows = -(-visits // 8) * 8
    rows = count * 4 * half // strips + pow_rows
    return pl.pallas_call(
        functools.partial(match_kernel, filters=filters, taps=taps, strips=strips, visits=visits),
        grid_spec=pltpu.PrefetchScalarGridSpec(
            num_scalar_prefetch=1,
            grid=(count,),
            in_specs=[
                pl.BlockSpec((1, length, length), lambda i, own: (i, 0, 0)),
                pl.BlockSpec((1,) + dtab.shape[1:], lambda i, own: (i, 0, 0)),
                pl.BlockSpec(taps_rev.shape, lambda i, own: (0, 0)),
                pl.BlockSpec((1,) + warp_taps.shape[1:], lambda i, own: (i, 0, 0)),
            ],
            out_specs=[pl.BlockSpec((rows, half), lambda i, own: (0, 0))] * strips,
            scratch_shapes=[
                pltpu.VMEM((length, filters * length), jnp.bfloat16),
                pltpu.VMEM((2, depth, length), jnp.bfloat16),
                pltpu.VMEM((2, 3 * half, depth), jnp.bfloat16),
                pltpu.VMEM((pow_rows, LANES), jnp.float32),
                pltpu.VMEM((4, half, half), jnp.float32),
            ],
        ),
        out_shape=[jax.ShapeDtypeStruct((rows, half), jnp.float32)] * strips,
        name="match_and_warp",
    )(own, images, dtab, taps_rev, warp_taps)


def coefficient_table(kernel_coeffs, col_taps, images, filters):
    taps = col_taps.shape[1]
    coeffs = kernel_coeffs.reshape(images, filters, filters, 6)
    cols = col_taps.astype(jnp.float32)
    mixed = jnp.sum(coeffs[..., None] * cols[None, :, None, None, :], axis=1)
    zero = jnp.zeros_like(mixed[:, :, 0])
    parts = [mixed[:, :, j] for j in range(6)]
    table = jnp.stack(
        [
            jnp.stack([parts[0], parts[2], parts[5]], axis=2),
            jnp.stack([parts[1], parts[4], zero], axis=2),
            jnp.stack([parts[3], zero, zero], axis=2),
        ],
        axis=1,
    )
    table = jnp.pad(table, ((0, 0), (0, 0), (0, 0), (0, 0), (0, SEG - taps)))
    table = table.reshape(images, 3, filters * 3 * SEG)
    extra = -table.shape[2] % LANES
    return jnp.pad(table, ((0, 0), (0, 0), (0, extra)))


def lanczos_taps(shifts):
    i = jnp.arange(LANES, dtype=jnp.float32)
    steps = jnp.stack([2.0 - i, i - 3.0])
    distance = steps + shifts[:, :, None]
    kernel = jnp.sinc(distance) * jnp.sinc(distance / 3.0)
    return jnp.where(jnp.abs(distance) < 3.0, kernel, 0.0)


def reversed_taps(row_taps):
    filters, taps = row_taps.shape
    flipped = row_taps[:, ::-1].astype(jnp.float32)
    return jnp.pad(flipped, ((0, -filters % 8), (0, LANES - taps)))


def reduce_kernel(own_ref, dest_ref, count_ref, *refs, strips, slots, images, visits, pixels, part, parts):
    pieces = refs[:strips]
    others = refs[strips:-4]
    out_ref, var_ref, acc0, acc1 = refs[-4:]
    pow_rows = var_ref.shape[0]
    height = out_ref.shape[0] // slots
    total = others[0][...]
    for other in others[1:]:
        total = total + other[...]
    total = jnp.sum(total, axis=1, keepdims=True)
    variance = jnp.broadcast_to(total / pixels + 1e-05, (pow_rows, LANES))
    var_ref[...] = variance
    weight = 1.0 / variance
    acc0[...] = jnp.zeros(acc0.shape, jnp.float32)
    acc1[...] = jnp.zeros(acc1.shape, jnp.float32)
    own = own_ref[0]
    for image in range(images):
        visit = image % visits
        scale = jnp.broadcast_to(weight[visit : visit + 1], (height, LANES))
        for k in range(strips):
            for block in range(4):
                item = 4 * image + block
                acc = acc0 if block % 2 == 0 else acc1
                slot = dest_ref[own ^ k, item]
                at = pl.ds(pl.multiple_of(slot * height, height), height)
                start = (item * parts + part) * height
                acc[at, :] = acc[at, :] + scale * pieces[k][start : start + height, :]
    for slot in range(slots):
        counts = count_ref[slot * pow_rows : (slot + 1) * pow_rows, :]
        denom = jnp.sum(counts * weight, axis=0, keepdims=True)
        inverse = 1.0 / jnp.where(denom > 0, denom, 1.0)
        at = slice(slot * height, (slot + 1) * height)
        out_ref[at, :] = (acc0[at, :] + acc1[at, :]) * inverse


def reduce_blocks(own, dest, counts, pieces, powers, slots, images, visits, pixels, part, parts):
    pow_rows = powers[0].shape[0]
    height = (pieces[0].shape[0] - pow_rows) // (images * 4 * parts)
    smem = pl.BlockSpec(memory_space=pltpu.SMEM)
    vmem = pl.BlockSpec(memory_space=pltpu.VMEM)
    kernel = functools.partial(
        reduce_kernel,
        strips=len(pieces),
        slots=slots,
        images=images,
        visits=visits,
        pixels=pixels,
        part=part,
        parts=parts,
    )
    return pl.pallas_call(
        kernel,
        in_specs=[smem, smem] + [vmem] * (1 + len(pieces) + len(powers)),
        out_specs=[vmem, vmem],
        out_shape=[
            jax.ShapeDtypeStruct((slots * height, LANES), jnp.float32),
            jax.ShapeDtypeStruct((pow_rows, LANES), jnp.float32),
        ],
        scratch_shapes=[pltpu.VMEM((slots * height, LANES), jnp.float32)] * 2,
        name="reduce_blocks",
    )(own, dest, counts, *pieces, *powers)


def finish_kernel(own_ref, dest_ref, var_ref, *refs, strips, visits, parts):
    warped = refs[:strips]
    templates = refs[strips:-1]
    out_ref = refs[-1]
    image = pl.program_id(0)
    height = out_ref.shape[2] // strips // parts
    scale = 1.0 / jnp.sqrt(var_ref[pl.ds(image % visits, 1), :])
    scale = jnp.broadcast_to(scale, (height, LANES))
    own = own_ref[0]
    for block in range(4):
        slot = dest_ref[own, 4 * image + block]
        at = pl.ds(pl.multiple_of(slot * height, height), height)
        for k in range(strips):
            strip = (own % strips) ^ k
            for part in range(parts):
                start = (block * parts + part) * height
                here = warped[k][start : start + height, :]
                rows = pl.ds(pl.multiple_of((strip * parts + part) * height, height), height)
                template = templates[k * parts + part][at, :]
                out_ref[0, block, rows, :] = (here - template) * scale


def finish(own, dest, variance, warped, templates, images, visits, parts):
    strips = len(warped)
    smem = pl.BlockSpec(memory_space=pltpu.SMEM)
    vmem = pl.BlockSpec(memory_space=pltpu.VMEM)
    per_image = (warped[0].shape[0] - variance.shape[0]) // images
    side = per_image // 4 * strips
    return pl.pallas_call(
        functools.partial(finish_kernel, strips=strips, visits=visits, parts=parts),
        grid=(images,),
        in_specs=[smem, smem, vmem]
        + [pl.BlockSpec((per_image, LANES), lambda i: (i, 0))] * strips
        + [vmem] * len(templates),
        out_specs=pl.BlockSpec((1, 4, side, LANES), lambda i: (i, 0, 0, 0)),
        out_shape=jax.ShapeDtypeStruct((images, 4, side, LANES), jnp.float32),
        name="finish",
    )(own, dest, variance, *warped, *templates)


GROUP = 8


def per_device(exposures, row_taps, col_taps, kernel_coeffs, subpixel, destination):
    tile_count, visits, length = exposures.shape[:3]
    filters, taps = row_taps.shape
    devices = lax.axis_size("tile")
    own = lax.axis_index("tile").astype(jnp.int32)
    images = tile_count * visits
    slots = tile_count * devices * 4
    pixels = tile_count * devices * length * length
    dest = destination.reshape(devices, images * 4)
    own_ref = own.reshape(1)

    def swap(x, k):
        return lax.ppermute(x, "tile", [(i, i ^ k) for i in range(devices)])

    def ahead(x, groups):
        shift = groups * GROUP
        return lax.ppermute(x, "tile", [(i, (i + shift) % devices) for i in range(devices)])

    hits = dest[:, :, None] == jnp.arange(slots, dtype=jnp.int32)
    counts = jnp.sum(
        hits.reshape(devices * tile_count, visits, 4, slots).astype(jnp.float32), axis=(0, 2)
    )
    pow_rows = -(-visits // 8) * 8
    counts = jnp.pad(counts.T, ((0, 0), (0, pow_rows - visits)))
    counts = jnp.broadcast_to(counts.reshape(slots * pow_rows, 1), (slots * pow_rows, LANES))

    warped = match_and_warp(
        own_ref % GROUP,
        exposures.reshape(images, length, length),
        coefficient_table(kernel_coeffs, col_taps, images, filters),
        reversed_taps(row_taps),
        lanczos_taps(subpixel.reshape(images, 2)),
        filters,
        taps,
        GROUP,
        visits,
    )
    pieces = [warped[0]] + [swap(warped[k], k) for k in range(1, GROUP)]
    power = pieces[0][-pow_rows:]
    for piece in pieces[1:]:
        power = power + piece[-pow_rows:]
    powers = [power] + [ahead(power, r) for r in range(1, devices // GROUP)]
    parts = 2
    full = {}
    for part in range(parts):
        partial, variance = reduce_blocks(
            own_ref, dest, counts, pieces, powers, slots, images, visits, pixels, part, parts
        )
        template = partial
        for r in range(1, devices // GROUP):
            template = template + ahead(partial, r)
        near = swap(template, 1)
        two = swap(template, 2)
        four = swap(template, 4)
        six = swap(two, 4) if part == 0 else swap(four, 2)
        full[part] = [template, near, two, swap(two, 1), four, swap(four, 1), six, swap(six, 1)]
    templates = [full[part][k] for k in range(GROUP) for part in range(parts)]
    result = finish(own_ref, dest, variance, warped, templates, images, visits, parts)
    return result.reshape(tile_count, visits, 4, BLOCK, BLOCK)


def solution(mesh):
    return jax.shard_map(
        per_device,
        mesh=mesh,
        in_specs=(
            P(("groups", "tile"), None, None, None),
            P(),
            P(),
            P(("groups", "tile"), None, None, None),
            P(("groups", "tile"), None, None),
            P("groups", None),
        ),
        out_specs=P(("groups", "tile"), None, None, None, None),
        check_vma=False,
    )
```

```python
import functools
import jax
import jax.numpy as jnp
from jax import lax
from jax.experimental import pallas as pl
from jax.experimental.pallas import tpu as pltpu
from jax.sharding import PartitionSpec as P


BLOCK = 128
LANES = 128
SEG = 32


def skew(rows8, base):
    base = base % LANES
    if base > LANES - 8:
        rows8 = pltpu.roll(rows8, 8, 1)
        base -= 8
    return pltpu.roll(rows8, base, 1, stride=1, stride_axis=0)


def iotas(rows):
    lane = lax.broadcasted_iota(jnp.int32, (rows, LANES), 1)
    row = lax.broadcasted_iota(jnp.int32, (rows, LANES), 0)
    return lane, lane - row


def split(x):
    high = x.astype(jnp.bfloat16)
    low = (x - high.astype(jnp.float32)).astype(jnp.bfloat16)
    return high, low


def banded_rows(tap_row, length, taps, first):
    _, diff = iotas(8)
    wide = jnp.broadcast_to(tap_row, (8, LANES))
    tiles = []
    for start in range(0, length, 8):
        rolled = skew(wide, start + first)
        cols = []
        for tile in range(length // LANES):
            k = diff + (LANES * tile - start - first)
            cols.append(jnp.where((k >= 0) & (k < taps), rolled, 0.0))
        tiles.append(jnp.concatenate(cols, axis=1) if len(cols) > 1 else cols[0])
    return jnp.concatenate(tiles, axis=0)


def as_column(row):
    count = row.shape[1]
    lane = lax.broadcasted_iota(jnp.int32, (count, count), 1)
    index = lax.broadcasted_iota(jnp.int32, (count, count), 0)
    return jnp.sum(jnp.where(lane == index, row, 0.0), axis=1, keepdims=True)


def sinc(x):
    angle = jnp.where(x == 0, 1.0, jnp.pi * x)
    return jnp.where(x == 0, 1.0, jnp.sin(angle) / angle)


def match_kernel(own_ref, x_ref, c_ref, rtap_ref, ctap_ref, sub_ref, *refs, strips, parts, visits):
    outs = refs[: strips * parts]
    rbig, s_win, h_win, powers, held, tap_rows, basis, table, shifts = refs[strips * parts :]
    filters, taps = rtap_ref.shape
    length = x_ref.shape[1]
    half = length // 2
    middle = taps // 2
    win = -(-(half + middle) // 16) * 16
    step = pl.program_id(0)

    @pl.when(step == 0)
    def _():
        tap_rows[...] = jnp.zeros(tap_rows.shape, jnp.float32)
        tap_rows[0:filters, 0:taps] = rtap_ref[...].astype(jnp.float32)
        tap_rows[8 : 8 + filters, 0:taps] = ctap_ref[...].astype(jnp.float32)
        i = lax.broadcasted_iota(jnp.int32, (LANES, LANES), 0)
        j = lax.broadcasted_iota(jnp.int32, (LANES, LANES), 1)
        flip = (i + j == taps - 1).astype(jnp.float32).astype(jnp.bfloat16)
        flipped = jnp.dot(
            tap_rows[0:8, :].astype(jnp.bfloat16), flip, preferred_element_type=jnp.float32
        )
        for b in range(filters):
            band = banded_rows(flipped[b : b + 1, :], length, taps, -middle)
            rbig[:, b * length : (b + 1) * length] = band.astype(jnp.bfloat16)
        s_win[...] = jnp.zeros(s_win.shape, jnp.bfloat16)
        h_win[...] = jnp.zeros(h_win.shape, jnp.bfloat16)
        powers[...] = jnp.zeros(powers.shape, jnp.float32)
        basis[...] = jnp.zeros(basis.shape, jnp.float32)
        for a in range(filters):
            row = jnp.broadcast_to(tap_rows[8 + a : 9 + a, :], (8, LANES))
            for b in range(filters):
                tile, off = divmod(b * SEG, LANES)
                moved = pltpu.roll(row, off, 1) if off else row
                basis[a * filters + b : a * filters + b + 1, tile * LANES : (tile + 1) * LANES] = (
                    moved[0:1]
                )
        lanes = lax.broadcasted_iota(jnp.int32, (1, LANES), 1).astype(jnp.float32)
        for axis, steps in enumerate((2.0 - lanes, lanes - 3.0)):
            distance = steps + as_column(sub_ref[axis : axis + 1, :])
            value = sinc(distance) * sinc(distance / 3.0)
            shifts[axis] = jnp.where(jnp.abs(distance) < 3.0, value, 0.0)
        count, terms = c_ref.shape[1:]
        for tile in range(basis.shape[1] // LANES):
            table[6 * tile : 6 * tile + 6] = jnp.dot(
                c_ref[...].reshape(6 * count, terms),
                basis[0:terms, tile * LANES : (tile + 1) * LANES],
                precision=lax.Precision.HIGHEST,
                preferred_element_type=jnp.float32,
            ).reshape(6, count, LANES)

    image = x_ref[0].astype(jnp.bfloat16)
    for b in range(filters):
        smooth = jnp.dot(
            image, rbig[:, b * length : (b + 1) * length], preferred_element_type=jnp.float32
        ).astype(jnp.bfloat16)
        s_win[0, b * win : (b + 1) * win, :] = smooth[0:win]
        s_win[1, b * win : (b + 1) * win, :] = smooth[length - win :]

    lane, diff = iotas(8)
    terms = [
        [
            jnp.broadcast_to(table[6 * tile + j, pl.ds(step, 1), :], (8, LANES))
            for j in range(6)
        ]
        for tile in range(basis.shape[1] // LANES)
    ]
    for side in range(2):
        origin = side * (length - win)
        for group in range(half // 16):
            halves = []
            for sub in range(2):
                start = 16 * group + 8 * sub
                row = lax.broadcasted_iota(jnp.int32, (8, LANES), 0) + (side * half + start)
                u = 2.0 * row.astype(jnp.float32) / (length - 1) - 1.0
                compact = {}
                for tile in range(basis.shape[1] // LANES):
                    t = terms[tile]
                    compact[0, tile] = t[0] + u * (t[1] + u * t[3])
                    compact[1, tile] = t[2] + u * t[4]
                    compact[2, tile] = t[5]
                acc = {}
                for b in range(filters):
                    lead = b * win + side * half + start - middle - origin
                    first = max(lead, b * win)
                    last = min(lead + 7 + taps - 1, (b + 1) * win - 1)
                    masks = {}
                    for tile in range(first // LANES, last // LANES + 1):
                        k = diff + (LANES * tile - lead)
                        mask = (k >= 0) & (k < taps)
                        if lead < b * win:
                            mask &= lane >= b * win - LANES * tile
                        if lead + 7 + taps > (b + 1) * win:
                            mask &= lane < (b + 1) * win - LANES * tile
                        masks[tile] = mask
                    source, off = divmod(b * SEG, LANES)
                    for q in range(3):
                        rolled = skew(compact[q, source], lead - off)
                        for tile, mask in masks.items():
                            acc[q, tile] = jnp.where(mask, rolled, acc.get((q, tile), 0.0))
                halves.append(acc)
            for q, tile in sorted(set(halves[0]) | set(halves[1])):
                zero = jnp.zeros((8, LANES), jnp.float32)
                both = jnp.concatenate([h.get((q, tile), zero) for h in halves], axis=0)
                h_win[
                    side,
                    q * half + 16 * group : q * half + 16 * group + 16,
                    tile * LANES : (tile + 1) * LANES,
                ] = both.astype(jnp.bfloat16)

    col = lax.broadcasted_iota(jnp.int32, (1, length), 1).astype(jnp.float32)
    w = 2.0 * col / (length - 1) - 1.0
    vertical = split(banded_rows(shifts[0, pl.ds(step, 1), :], half, 6, -2))
    horizontal = split(banded_rows(shifts[1, pl.ds(step, 1), :], half, 6, -3))
    left = jnp.concatenate([vertical[0], vertical[0], vertical[1]], axis=1)
    right = jnp.concatenate([horizontal[0], horizontal[0], horizontal[1]], axis=0)
    power = jnp.zeros((1, LANES), jnp.float32)
    for side in range(2):
        z = jnp.dot(h_win[side], s_win[side], preferred_element_type=jnp.float32)
        matched = z[0:half] + w * (z[half : 2 * half] + w * z[2 * half :])
        squares = jnp.sum(matched * matched, axis=0, keepdims=True)
        power += squares[:, :half] + squares[:, half:]
        high, low = split(matched)
        stacked = jnp.concatenate([high, low, high], axis=0)
        moved = jnp.dot(left, stacked, preferred_element_type=jnp.float32)
        for c in range(2):
            high, low = split(moved[:, c * half : (c + 1) * half])
            lhs = jnp.concatenate([high, low, high], axis=1)
            held[2 * side + c] = jnp.dot(lhs, right, preferred_element_type=jnp.float32)
    visit = pl.ds(step % visits, 1)
    powers[visit, :] = powers[visit, :] + power
    height = half // strips // parts
    for k in range(strips):
        for part in range(parts):
            begin = ((own_ref[0] ^ k) * parts + part) * height
            rows = pl.ds(pl.multiple_of(begin, height), height)
            out = outs[k * parts + part]
            for block in range(4):
                at = pl.ds(pl.multiple_of((4 * step + block) * height, height), height)
                out[at, :] = held[block, rows, :]

    @pl.when(step == pl.num_programs(0) - 1)
    def _():
        for k in range(strips):
            out = outs[k * parts]
            out[out.shape[0] - powers.shape[0] :, :] = powers[...]


def match_and_warp(own, images, coeffs, row_taps, col_taps, subpixel, strips, parts, visits):
    count, length, _ = images.shape
    filters, taps = row_taps.shape
    half = length // 2
    win = -(-(half + taps // 2) // 16) * 16
    depth = -(-filters * win // LANES) * LANES
    pow_rows = -(-visits // 8) * 8
    rows = count * 4 * half // strips // parts
    shapes = []
    for _ in range(strips):
        for part in range(parts):
            extra = pow_rows if part == 0 else 0
            shapes.append(jax.ShapeDtypeStruct((rows + extra, half), jnp.float32))
    return pl.pallas_call(
        functools.partial(match_kernel, strips=strips, parts=parts, visits=visits),
        grid_spec=pltpu.PrefetchScalarGridSpec(
            num_scalar_prefetch=1,
            grid=(count,),
            in_specs=[
                pl.BlockSpec((1, length, length), lambda i, own: (i, 0, 0)),
                pl.BlockSpec(coeffs.shape, lambda i, own: (0, 0, 0)),
                pl.BlockSpec(row_taps.shape, lambda i, own: (0, 0)),
                pl.BlockSpec(col_taps.shape, lambda i, own: (0, 0)),
                pl.BlockSpec(subpixel.shape, lambda i, own: (0, 0)),
            ],
            out_specs=[pl.BlockSpec(s.shape, lambda i, own: (0, 0)) for s in shapes],
            scratch_shapes=[
                pltpu.VMEM((length, filters * length), jnp.bfloat16),
                pltpu.VMEM((2, depth, length), jnp.bfloat16),
                pltpu.VMEM((2, 3 * half, depth), jnp.bfloat16),
                pltpu.VMEM((pow_rows, LANES), jnp.float32),
                pltpu.VMEM((4, half, half), jnp.float32),
                pltpu.VMEM((16, LANES), jnp.float32),
                pltpu.VMEM((-(-filters * filters // 8) * 8, -(-filters * SEG // LANES) * LANES), jnp.float32),
                pltpu.VMEM((6 * -(-filters * SEG // LANES), count, LANES), jnp.float32),
                pltpu.VMEM((2, count, LANES), jnp.float32),
            ],
        ),
        out_shape=shapes,
        name="match_and_warp",
    )(own, images, coeffs, row_taps, col_taps, subpixel)


def reduce_kernel(own_ref, dest_ref, slot_ref, *refs, strips, slots, images, visits, pixels):
    pieces = refs[:strips]
    others = refs[strips:-4]
    out_ref, var_ref, acc0, acc1 = refs[-4:]
    pow_rows = var_ref.shape[0]
    height = out_ref.shape[0] // slots
    total = others[0][...]
    for other in others[1:]:
        total = total + other[...]
    total = jnp.sum(total, axis=1, keepdims=True)
    variance = jnp.broadcast_to(total / pixels + 1e-05, (pow_rows, LANES))
    var_ref[...] = variance
    weight = 1.0 / variance
    acc0[...] = jnp.zeros(acc0.shape, jnp.float32)
    acc1[...] = jnp.zeros(acc1.shape, jnp.float32)
    own = own_ref[0]
    for image in range(images):
        visit = image % visits
        scale = jnp.broadcast_to(weight[visit : visit + 1], (height, LANES))
        for k in range(strips):
            for block in range(4):
                item = 4 * image + block
                acc = acc0 if block % 2 == 0 else acc1
                slot = dest_ref[own ^ k, item]
                at = pl.ds(pl.multiple_of(slot * height, height), height)
                rows = slice(item * height, (item + 1) * height)
                acc[at, :] = acc[at, :] + scale * pieces[k][rows, :]
    devices, items = slot_ref.shape
    lane = lax.broadcasted_iota(jnp.int32, (pow_rows, items), 1)
    row = lax.broadcasted_iota(jnp.int32, (pow_rows, items), 0)
    by_item = jnp.sum(
        jnp.where(lane // 4 % visits == row, weight[:, 0:1], 0.0), axis=0, keepdims=True
    )
    index = lax.broadcasted_iota(jnp.int32, (slots, items), 0)
    hits = jnp.zeros((slots, items), jnp.float32)
    for device in range(devices):
        hits = hits + jnp.where(slot_ref[device : device + 1, :] == index, 1.0, 0.0)
    denom = jnp.sum(hits * by_item, axis=1, keepdims=True)
    inverse = 1.0 / jnp.where(denom > 0, denom, 1.0)
    for slot in range(slots):
        at = slice(slot * height, (slot + 1) * height)
        scale = jnp.broadcast_to(inverse[slot : slot + 1, :], (height, LANES))
        out_ref[at, :] = (acc0[at, :] + acc1[at, :]) * scale


def reduce_blocks(own, dest, pieces, powers, slots, images, visits, pixels):
    pow_rows = powers[0].shape[0]
    height = pieces[0].shape[0] // (images * 4)
    smem = pl.BlockSpec(memory_space=pltpu.SMEM)
    vmem = pl.BlockSpec(memory_space=pltpu.VMEM)
    kernel = functools.partial(
        reduce_kernel,
        strips=len(pieces),
        slots=slots,
        images=images,
        visits=visits,
        pixels=pixels,
    )
    return pl.pallas_call(
        kernel,
        in_specs=[smem, smem] + [vmem] * (1 + len(pieces) + len(powers)),
        out_specs=[vmem, vmem],
        out_shape=[
            jax.ShapeDtypeStruct((slots * height, LANES), jnp.float32),
            jax.ShapeDtypeStruct((pow_rows, LANES), jnp.float32),
        ],
        scratch_shapes=[pltpu.VMEM((slots * height, LANES), jnp.float32)] * 2,
        name="reduce_blocks",
    )(own, dest, dest, *pieces, *powers)


def finish_kernel(own_ref, dest_ref, var_ref, *refs, visits, parts):
    warped = refs[: 2 * parts]
    templates = refs[2 * parts : 4 * parts]
    out_ref = refs[-1]
    own = own_ref[0]
    image_count = out_ref.shape[0]
    height = out_ref.shape[2] // 2 // parts
    inverse = 1.0 / jnp.sqrt(var_ref[...])
    for image in range(image_count):
        visit = image % visits
        scale = jnp.broadcast_to(inverse[visit : visit + 1, :], (height, LANES))
        for block in range(4):
            item = 4 * image + block
            slot = dest_ref[own, item]
            at = pl.ds(pl.multiple_of(slot * height, height), height)
            for k in range(2):
                for part in range(parts):
                    here = warped[k * parts + part][item * height : (item + 1) * height, :]
                    template = templates[k * parts + part][at, :]
                    begin = (((own & 1) ^ k) * parts + part) * height
                    rows = pl.ds(pl.multiple_of(begin, height), height)
                    out_ref[image, block, rows, :] = (here - template) * scale


def finish(own, dest, variance, warped, templates, previous, pair, strips, images, visits, parts):
    height = warped[1].shape[0] // (images * 4)
    side = height * parts * strips
    smem = pl.BlockSpec(memory_space=pltpu.SMEM)

    def whole(x):
        return pl.BlockSpec(x.shape, lambda i, own: (0, 0))

    extra = [] if previous is None else [previous]
    inputs = [variance, *warped, *templates]
    return pl.pallas_call(
        functools.partial(finish_kernel, visits=visits, parts=parts),
        grid_spec=pltpu.PrefetchScalarGridSpec(
            num_scalar_prefetch=1,
            grid=(1,),
            in_specs=[smem]
            + [whole(x) for x in inputs]
            + [pl.BlockSpec(memory_space=pl.ANY) for _ in extra],
            out_specs=pl.BlockSpec(
                (images, 4, 2 * height * parts, LANES),
                lambda i, own: (0, 0, (own[0] % strips // 2) ^ (pair // 2), 0),
            ),
        ),
        out_shape=jax.ShapeDtypeStruct((images, 4, side, LANES), jnp.float32),
        input_output_aliases={2 + len(inputs): 0} if extra else {},
        name="finish",
    )(own, dest, *inputs, *extra)


GROUP = 8
PARTS = 2


def per_device(exposures, row_taps, col_taps, kernel_coeffs, subpixel, destination):
    tile_count, visits, length = exposures.shape[:3]
    filters, _ = row_taps.shape
    devices = lax.axis_size("tile")
    own = lax.axis_index("tile").astype(jnp.int32).reshape(1)
    images = tile_count * visits
    slots = tile_count * devices * 4
    pixels = tile_count * devices * length * length
    dest = destination.reshape(devices, images * 4)

    def permute(x, target):
        return lax.ppermute(x, "tile", [(i, target(i)) for i in range(devices)])

    def swap(x, k):
        return permute(x, lambda i: i ^ k)

    def ahead(x, groups):
        return permute(x, lambda i: (i + groups * GROUP) % devices)

    warped = match_and_warp(
        own % GROUP,
        exposures.reshape(images, length, length),
        kernel_coeffs.transpose(3, 0, 1, 2).reshape(-1, images, filters * filters),
        row_taps,
        col_taps,
        subpixel.transpose(2, 0, 1).reshape(2, images),
        GROUP,
        PARTS,
        visits,
    )
    others = devices // GROUP
    pow_rows = -(-visits // 8) * 8
    full = []
    pieces = []
    for part in range(PARTS):
        mine = [warped[k * PARTS + part] for k in range(GROUP)]
        pieces.append([mine[0]] + [swap(mine[k], k) for k in range(1, GROUP)])
    power = pieces[0][0][-pow_rows:]
    for piece in pieces[0][1:]:
        power = power + piece[-pow_rows:]
    powers = [power] + [ahead(power, r) for r in range(1, others)]
    for part in range(PARTS):
        partial, variance = reduce_blocks(
            own, dest, pieces[part], powers, slots, images, visits, pixels
        )
        moved = [ahead(partial, r) for r in range(1, others)]
        template = partial
        for piece in moved:
            template = template + piece
        two = swap(template, 2)
        four = swap(template, 4)
        six = swap(two, 4) if part == 0 else swap(four, 2)
        full.append(
            [template, swap(template, 1)]
            + [two, swap(two, 1)]
            + [four, swap(four, 1)]
            + [six, swap(six, 1)]
        )
    result = None
    for pair in range(0, GROUP, 2):
        keys = [(k, part) for k in (pair, pair + 1) for part in range(PARTS)]
        result = finish(
            own,
            dest,
            variance,
            [warped[k * PARTS + part] for k, part in keys],
            [full[part][k] for k, part in keys],
            result,
            pair,
            GROUP,
            images,
            visits,
            PARTS,
        )
    return result.reshape(tile_count, visits, 4, BLOCK, BLOCK)


def solution(mesh):
    return jax.shard_map(
        per_device,
        mesh=mesh,
        in_specs=(
            P(("groups", "tile"), None, None, None),
            P(),
            P(),
            P(("groups", "tile"), None, None, None),
            P(("groups", "tile"), None, None),
            P("groups", None),
        ),
        out_specs=P(("groups", "tile"), None, None, None, None),
        check_vma=False,
    )
```

```python
import functools
import jax
import jax.numpy as jnp
from jax import lax
from jax.experimental import pallas as pl
from jax.experimental.pallas import tpu as pltpu
from jax.sharding import PartitionSpec as P


BLOCK = 128
LANES = 128
SEG = 32


def skew(rows8, base):
    base = base % LANES
    if base > LANES - 8:
        rows8 = pltpu.roll(rows8, 8, 1)
        base -= 8
    return pltpu.roll(rows8, base, 1, stride=1, stride_axis=0)


def iotas(rows):
    lane = lax.broadcasted_iota(jnp.int32, (rows, LANES), 1)
    row = lax.broadcasted_iota(jnp.int32, (rows, LANES), 0)
    return lane, lane - row


def split(x):
    high = x.astype(jnp.bfloat16)
    low = (x - high.astype(jnp.float32)).astype(jnp.bfloat16)
    return high, low


def banded_rows(tap_row, length, taps, first):
    _, diff = iotas(8)
    wide = jnp.broadcast_to(tap_row, (8, LANES))
    tiles = []
    for start in range(0, length, 8):
        rolled = skew(wide, start + first)
        cols = []
        for tile in range(length // LANES):
            k = diff + (LANES * tile - start - first)
            cols.append(jnp.where((k >= 0) & (k < taps), rolled, 0.0))
        tiles.append(jnp.concatenate(cols, axis=1) if len(cols) > 1 else cols[0])
    return jnp.concatenate(tiles, axis=0)


def as_column(row):
    count = row.shape[1]
    lane = lax.broadcasted_iota(jnp.int32, (count, count), 1)
    index = lax.broadcasted_iota(jnp.int32, (count, count), 0)
    return jnp.sum(jnp.where(lane == index, row, 0.0), axis=1, keepdims=True)


def sinc(x):
    angle = jnp.where(x == 0, 1.0, jnp.pi * x)
    return jnp.where(x == 0, 1.0, jnp.sin(angle) / angle)


def banded_region(tap_row, rows, width, taps, first, offset, span):
    lane, diff = iotas(8)
    wide = jnp.broadcast_to(tap_row, (8, LANES))
    chunks = []
    for start in range(0, rows, 8):
        lead = start + first + offset
        rolled = skew(wide, lead)
        cols = []
        for tile in range(width // LANES):
            begin = LANES * tile
            k = diff + (begin - lead)
            keep = (k >= 0) & (k < taps) & (lane >= offset - begin) & (lane < offset + span - begin)
            cols.append(jnp.where(keep, rolled, 0.0))
        chunks.append(jnp.concatenate(cols, axis=1))
    return jnp.concatenate(chunks, axis=0)


def fill_matched_coefficients(step, table, h_win, side, filters, taps, length, win):
    half = length // 2
    middle = taps // 2
    origin = side * (length - win)
    lane, diff = iotas(8)
    tiles = -(-filters * SEG // LANES)
    terms = [
        [jnp.broadcast_to(table[6 * t + j, pl.ds(step, 1), :], (8, LANES)) for j in range(6)]
        for t in range(tiles)
    ]
    for group in range(half // 16):
        halves = []
        for sub in range(2):
            start = 16 * group + 8 * sub
            row = lax.broadcasted_iota(jnp.int32, (8, LANES), 0) + (side * half + start)
            u = 2.0 * row.astype(jnp.float32) / (length - 1) - 1.0
            compact = {}
            for tile in range(tiles):
                t = terms[tile]
                compact[0, tile] = t[0] + u * (t[1] + u * t[3])
                compact[1, tile] = t[2] + u * t[4]
                compact[2, tile] = t[5]
            acc = {}
            for b in range(filters):
                lead = b * win + side * half + start - middle - origin
                first = max(lead, b * win)
                last = min(lead + 7 + taps - 1, (b + 1) * win - 1)
                masks = {}
                for tile in range(first // LANES, last // LANES + 1):
                    k = diff + (LANES * tile - lead)
                    mask = (k >= 0) & (k < taps)
                    if lead < b * win:
                        mask &= lane >= b * win - LANES * tile
                    if lead + 7 + taps > (b + 1) * win:
                        mask &= lane < (b + 1) * win - LANES * tile
                    masks[tile] = mask
                source, off = divmod(b * SEG, LANES)
                for q in range(3):
                    rolled = skew(compact[q, source], lead - off)
                    for tile, mask in masks.items():
                        acc[q, tile] = jnp.where(mask, rolled, acc.get((q, tile), 0.0))
            halves.append(acc)
        for q, tile in sorted(set(halves[0]) | set(halves[1])):
            zero = jnp.zeros((8, LANES), jnp.float32)
            both = jnp.concatenate([h.get((q, tile), zero) for h in halves], axis=0)
            h_win[
                side,
                q * half + 16 * group : q * half + 16 * group + 16,
                tile * LANES : (tile + 1) * LANES,
            ] = both.astype(jnp.bfloat16)


def match_kernel(x_ref, c_ref, rtap_ref, ctap_ref, out_ref, pow_ref, *refs, pack, visits):
    rbig, tap_rows, basis, table = refs[:4]
    s_wins = refs[4 : 4 + pack]
    h_wins = refs[4 + pack :]
    filters, taps = rtap_ref.shape
    length = x_ref.shape[1]
    half = length // 2
    middle = taps // 2
    win = -(-(half + middle) // 16) * 16
    step = pl.program_id(0)

    @pl.when(step == 0)
    def _():
        tap_rows[...] = jnp.zeros(tap_rows.shape, jnp.float32)
        tap_rows[0:filters, 0:taps] = rtap_ref[...].astype(jnp.float32)
        tap_rows[8 : 8 + filters, 0:taps] = ctap_ref[...].astype(jnp.float32)
        i = lax.broadcasted_iota(jnp.int32, (LANES, LANES), 0)
        j = lax.broadcasted_iota(jnp.int32, (LANES, LANES), 1)
        flip = (i + j == taps - 1).astype(jnp.float32).astype(jnp.bfloat16)
        flipped = jnp.dot(
            tap_rows[0:8, :].astype(jnp.bfloat16), flip, preferred_element_type=jnp.float32
        )
        for b in range(filters):
            band = banded_rows(flipped[b : b + 1, :], length, taps, -middle)
            rbig[:, b * length : (b + 1) * length] = band.astype(jnp.bfloat16)
        for ref in (*s_wins, *h_wins):
            ref[...] = jnp.zeros(ref.shape, jnp.bfloat16)
        pow_ref[...] = jnp.zeros(pow_ref.shape, jnp.float32)
        basis[...] = jnp.zeros(basis.shape, jnp.float32)
        for a in range(filters):
            row = jnp.broadcast_to(tap_rows[8 + a : 9 + a, :], (8, LANES))
            for b in range(filters):
                tile, off = divmod(b * SEG, LANES)
                moved = pltpu.roll(row, off, 1) if off else row
                basis[a * filters + b : a * filters + b + 1, tile * LANES : (tile + 1) * LANES] = (
                    moved[0:1]
                )
        count, terms = c_ref.shape[1:]
        for tile in range(basis.shape[1] // LANES):
            table[6 * tile : 6 * tile + 6] = jnp.dot(
                c_ref[...].reshape(6 * count, terms),
                basis[0:terms, tile * LANES : (tile + 1) * LANES],
                precision=lax.Precision.HIGHEST,
                preferred_element_type=jnp.float32,
            ).reshape(6, count, LANES)

    col = lax.broadcasted_iota(jnp.int32, (1, length), 1).astype(jnp.float32)
    w = 2.0 * col / (length - 1) - 1.0

    def smooth(n):
        image = x_ref[n].astype(jnp.bfloat16)
        for b in range(filters):
            part = jnp.dot(
                image, rbig[:, b * length : (b + 1) * length], preferred_element_type=jnp.float32
            ).astype(jnp.bfloat16)
            s_wins[n][0, b * win : (b + 1) * win, :] = part[0:win]
            s_wins[n][1, b * win : (b + 1) * win, :] = part[length - win :]

    def fill(n, side):
        fill_matched_coefficients(
            step * pack + n, table, h_wins[n], side, filters, taps, length, win
        )

    def combine(n, side):
        z = jnp.dot(h_wins[n][side], s_wins[n][side], preferred_element_type=jnp.float32)
        matched = z[0:half] + w * (z[half : 2 * half] + w * z[2 * half :])
        out_ref[n, side * half : (side + 1) * half, :] = matched
        squares = jnp.sum(matched * matched, axis=0, keepdims=True)
        visit = pl.ds((step * pack + n) % visits, 1)
        pow_ref[visit, :] = pow_ref[visit, :] + (squares[:, :half] + squares[:, half:])

    smooth(0)
    fill(0, 0)
    for n in range(pack):
        if n + 1 < pack:
            smooth(n + 1)
        fill(n, 1)
        combine(n, 0)
        if n + 1 < pack:
            fill(n + 1, 0)
        combine(n, 1)


def match(images, coeffs, row_taps, col_taps, visits):
    count, length, _ = images.shape
    filters, taps = row_taps.shape
    half = length // 2
    win = -(-(half + taps // 2) // 16) * 16
    depth = -(-filters * win // LANES) * LANES
    pow_rows = -(-visits // 8) * 8
    pack = 2 - count % 2
    tiles = -(-filters * SEG // LANES)
    return pl.pallas_call(
        functools.partial(match_kernel, pack=pack, visits=visits),
        grid=(count // pack,),
        in_specs=[
            pl.BlockSpec((pack, length, length), lambda i: (i, 0, 0)),
            pl.BlockSpec(coeffs.shape, lambda i: (0, 0, 0)),
            pl.BlockSpec(row_taps.shape, lambda i: (0, 0)),
            pl.BlockSpec(col_taps.shape, lambda i: (0, 0)),
        ],
        out_specs=[
            pl.BlockSpec((pack, length, length), lambda i: (i, 0, 0)),
            pl.BlockSpec((pow_rows, LANES), lambda i: (0, 0)),
        ],
        out_shape=[
            jax.ShapeDtypeStruct((count, length, length), jnp.float32),
            jax.ShapeDtypeStruct((pow_rows, LANES), jnp.float32),
        ],
        scratch_shapes=[
            pltpu.VMEM((length, filters * length), jnp.bfloat16),
            pltpu.VMEM((16, LANES), jnp.float32),
            pltpu.VMEM((-(-filters * filters // 8) * 8, tiles * LANES), jnp.float32),
            pltpu.VMEM((6 * tiles, count, LANES), jnp.float32),
        ]
        + [pltpu.VMEM((2, depth, length), jnp.bfloat16)] * pack
        + [pltpu.VMEM((2, 3 * half, depth), jnp.bfloat16)] * pack,
        name="match",
    )(images, coeffs, row_taps, col_taps)


def warp_kernel(own_ref, sub_ref, m_ref, *refs, strips, part, parts, pack, powers):
    given = refs[:powers]
    outs = refs[powers : powers + strips]
    shifts, held = refs[powers + strips :]
    step = pl.program_id(0)
    half = m_ref.shape[1] // 2
    rows = half // parts
    height = rows // strips
    low = max(part * rows - 3, 0) // 16 * 16
    span = min(-(-(part * rows + rows + 2) // 16) * 16, half) - low
    depth = -(-3 * span // LANES) * LANES

    @pl.when(step == 0)
    def _():
        lanes = lax.broadcasted_iota(jnp.int32, (1, LANES), 1).astype(jnp.float32)
        for axis, steps in enumerate((2.0 - lanes, lanes - 3.0)):
            distance = steps + as_column(sub_ref[axis : axis + 1, :])
            value = sinc(distance) * sinc(distance / 3.0)
            shifts[axis] = jnp.where(jnp.abs(distance) < 3.0, value, 0.0)

    lane = lax.broadcasted_iota(jnp.int32, (1, depth), 1)
    for n in range(pack):
        image = step * pack + n
        left = jnp.zeros((rows, depth), jnp.float32)
        for copy in range(3):
            left += banded_region(
                shifts[0, pl.ds(image, 1), :], rows, depth, 6, part * rows - low - 2, copy * span, span
            )
        high = left.astype(jnp.bfloat16).astype(jnp.float32)
        left = jnp.where(lane < 2 * span, high, left - high).astype(jnp.bfloat16)
        horizontal = split(banded_rows(shifts[1, pl.ds(image, 1), :], half, 6, -3))
        right = jnp.concatenate([horizontal[0], horizontal[0], horizontal[1]], axis=0)
        moved = []
        for side in range(2):
            upper, lower = split(m_ref[n, side * half + low : side * half + low + span, :])
            stacked = [upper, lower, upper]
            if depth > 3 * span:
                stacked.append(jnp.zeros((depth - 3 * span, 2 * half), jnp.bfloat16))
            full = jnp.dot(
                left, jnp.concatenate(stacked, axis=0), preferred_element_type=jnp.float32
            )
            moved += [full[:, :half], full[:, half:]]
        upper, lower = split(jnp.concatenate(moved, axis=0))
        lhs = jnp.concatenate([upper, lower, upper], axis=1)
        held[n] = jnp.dot(lhs, right, preferred_element_type=jnp.float32).reshape(4, rows, half)
    for n in range(pack):
        for k in range(strips):
            begin = pl.ds(pl.multiple_of((own_ref[0] ^ k) * height, height), height)
            for block in range(4):
                item = 4 * (step * pack + n) + block
                at = pl.ds(pl.multiple_of(item * height, height), height)
                outs[k][at, :] = held[n, block, begin, :]

    if powers:

        @pl.when(step == pl.num_programs(0) - 1)
        def _():
            total = given[0][...]
            for other in given[1:]:
                total = total + other[...]
            for out in outs:
                out[out.shape[0] - total.shape[0] :, :] = total


def warp(own, subpixel, matched, powers, part, parts, strips):
    count, length, _ = matched.shape
    half = length // 2
    rows = count * 4 * half // strips // parts + sum(p.shape[0] for p in powers[:1])
    pack = 2 - count % 2
    return pl.pallas_call(
        functools.partial(
            warp_kernel, strips=strips, part=part, parts=parts, pack=pack, powers=len(powers)
        ),
        grid_spec=pltpu.PrefetchScalarGridSpec(
            num_scalar_prefetch=1,
            grid=(count // pack,),
            in_specs=[
                pl.BlockSpec(subpixel.shape, lambda i, own: (0, 0)),
                pl.BlockSpec((pack, length, length), lambda i, own: (i, 0, 0)),
            ]
            + [pl.BlockSpec(p.shape, lambda i, own: (0, 0)) for p in powers],
            out_specs=[pl.BlockSpec((rows, half), lambda i, own: (0, 0))] * strips,
            scratch_shapes=[
                pltpu.VMEM((2, count, LANES), jnp.float32),
                pltpu.VMEM((pack, 4, half // parts, half), jnp.float32),
            ],
        ),
        out_shape=[jax.ShapeDtypeStruct((rows, half), jnp.float32)] * strips,
        name="warp",
    )(own, subpixel, matched, *powers)


def reduce_kernel(own_ref, dest_ref, slot_ref, *refs, strips, slots, images, visits, pixels):
    pieces = refs[:strips]
    given = refs[strips:-4]
    out_ref, var_ref, acc0, acc1 = refs[-4:]
    pow_rows = var_ref.shape[0]
    height = out_ref.shape[0] // slots
    if given:
        variance = given[0][...]
    else:
        total = pieces[0][pieces[0].shape[0] - pow_rows :, :]
        for piece in pieces[1:]:
            total = total + piece[piece.shape[0] - pow_rows :, :]
        total = jnp.sum(total, axis=1, keepdims=True)
        variance = jnp.broadcast_to(total / pixels + 1e-05, (pow_rows, LANES))
    var_ref[...] = variance
    weight = 1.0 / variance
    acc0[...] = jnp.zeros(acc0.shape, jnp.float32)
    acc1[...] = jnp.zeros(acc1.shape, jnp.float32)
    own = own_ref[0]
    for image in range(images):
        visit = image % visits
        scale = jnp.broadcast_to(weight[visit : visit + 1], (height, LANES))
        for k in range(strips):
            for block in range(4):
                item = 4 * image + block
                acc = acc0 if block % 2 == 0 else acc1
                slot = dest_ref[own ^ k, item]
                at = pl.ds(pl.multiple_of(slot * height, height), height)
                rows = slice(item * height, (item + 1) * height)
                acc[at, :] = acc[at, :] + scale * pieces[k][rows, :]
    devices, items = slot_ref.shape
    lane = lax.broadcasted_iota(jnp.int32, (pow_rows, items), 1)
    row = lax.broadcasted_iota(jnp.int32, (pow_rows, items), 0)
    by_item = jnp.sum(
        jnp.where(lane // 4 % visits == row, weight[:, 0:1], 0.0), axis=0, keepdims=True
    )
    index = lax.broadcasted_iota(jnp.int32, (slots, items), 0)
    hits = jnp.zeros((slots, items), jnp.float32)
    for device in range(devices):
        hits = hits + jnp.where(slot_ref[device : device + 1, :] == index, 1.0, 0.0)
    denom = jnp.sum(hits * by_item, axis=1, keepdims=True)
    inverse = 1.0 / jnp.where(denom > 0, denom, 1.0)
    for slot in range(slots):
        at = slice(slot * height, (slot + 1) * height)
        scale = jnp.broadcast_to(inverse[slot : slot + 1, :], (height, LANES))
        out_ref[at, :] = (acc0[at, :] + acc1[at, :]) * scale


def reduce_blocks(own, dest, pieces, variance, slots, images, visits, pixels):
    pow_rows = -(-visits // 8) * 8
    given = [] if variance is None else [variance]
    height = pieces[0].shape[0] // (images * 4)
    smem = pl.BlockSpec(memory_space=pltpu.SMEM)
    vmem = pl.BlockSpec(memory_space=pltpu.VMEM)
    kernel = functools.partial(
        reduce_kernel,
        strips=len(pieces),
        slots=slots,
        images=images,
        visits=visits,
        pixels=pixels,
    )
    return pl.pallas_call(
        kernel,
        in_specs=[smem, smem] + [vmem] * (1 + len(pieces) + len(given)),
        out_specs=[vmem, vmem],
        out_shape=[
            jax.ShapeDtypeStruct((slots * height, LANES), jnp.float32),
            jax.ShapeDtypeStruct((pow_rows, LANES), jnp.float32),
        ],
        scratch_shapes=[pltpu.VMEM((slots * height, LANES), jnp.float32)] * 2,
        name="reduce_blocks",
    )(own, dest, dest, *pieces, *given)


def finish_kernel(own_ref, dest_ref, var_ref, *refs, strips, visits):
    warped = refs[:strips]
    templates = refs[strips : 2 * strips]
    out_ref = refs[-1]
    own = own_ref[0]
    height = out_ref.shape[2] // strips
    inverse = 1.0 / jnp.sqrt(var_ref[...])
    for image in range(out_ref.shape[0]):
        visit = image % visits
        scale = jnp.broadcast_to(inverse[visit : visit + 1, :], (height, LANES))
        for block in range(4):
            item = 4 * image + block
            at = pl.ds(pl.multiple_of(dest_ref[own, item] * height, height), height)
            for k in range(strips):
                here = warped[k][item * height : (item + 1) * height, :]
                rows = pl.ds(pl.multiple_of(((own % strips) ^ k) * height, height), height)
                out_ref[image, block, rows, :] = (here - templates[k][at, :]) * scale


def finish(own, dest, variance, warped, templates, previous, part, images, visits):
    strips = len(warped)
    smem = pl.BlockSpec(memory_space=pltpu.SMEM)
    vmem = pl.BlockSpec(memory_space=pltpu.VMEM)
    extra = [] if previous is None else [previous]
    inputs = [variance, *warped, *templates]
    return pl.pallas_call(
        functools.partial(finish_kernel, strips=strips, visits=visits),
        grid=(1,),
        in_specs=[smem, smem]
        + [vmem] * len(inputs)
        + [pl.BlockSpec(memory_space=pl.ANY) for _ in extra],
        out_specs=pl.BlockSpec((images, 4, BLOCK // PARTS, LANES), lambda i: (0, 0, part, 0)),
        out_shape=jax.ShapeDtypeStruct((images, 4, BLOCK, LANES), jnp.float32),
        input_output_aliases={2 + len(inputs): 0} if extra else {},
        name="finish",
    )(own, dest, *inputs, *extra)


GROUP = 8
PARTS = 2


def per_device(exposures, row_taps, col_taps, kernel_coeffs, subpixel, destination):
    tile_count, visits, length = exposures.shape[:3]
    filters, _ = row_taps.shape
    devices = lax.axis_size("tile")
    own = lax.axis_index("tile").astype(jnp.int32).reshape(1)
    images = tile_count * visits
    slots = tile_count * devices * 4
    pixels = tile_count * devices * length * length
    dest = destination.reshape(devices, images * 4)

    def permute(x, target):
        return lax.ppermute(x, "tile", [(i, target(i)) for i in range(devices)])

    def swap(x, k):
        return permute(x, lambda i: i ^ k)

    def ahead(x, groups):
        return permute(x, lambda i: (i + groups * GROUP) % devices)

    others = devices // GROUP
    matched, power = match(
        exposures.reshape(images, length, length),
        kernel_coeffs.transpose(3, 0, 1, 2).reshape(-1, images, filters * filters),
        row_taps,
        col_taps,
        visits,
    )
    powers = [power] + [ahead(power, r) for r in range(1, others)]
    shifts = subpixel.transpose(2, 0, 1).reshape(2, images)
    warped = []
    pieces = []
    for part in range(PARTS):
        mine = warp(
            own % GROUP, shifts, matched, [] if part else powers, part, PARTS, GROUP
        )
        warped.append(mine)
        pieces.append([mine[0]] + [swap(mine[k], k) for k in range(1, GROUP)])
    full = []
    variance = None
    for part in range(PARTS):
        partial, variance = reduce_blocks(
            own, dest, pieces[part], variance, slots, images, visits, pixels
        )
        moved = [ahead(partial, r) for r in range(1, others)]
        template = partial
        for piece in moved:
            template = template + piece
        two = swap(template, 2)
        four = swap(template, 4)
        six = swap(template, 6)
        full.append(
            [template, swap(template, 1)]
            + [two, swap(two, 1)]
            + [four, swap(four, 1)]
            + [six, swap(six, 1)]
        )
    result = None
    for part in range(PARTS):
        result = finish(own, dest, variance, warped[part], full[part], result, part, images, visits)
    return result.reshape(tile_count, visits, 4, BLOCK, BLOCK)


def solution(mesh):
    return jax.shard_map(
        per_device,
        mesh=mesh,
        in_specs=(
            P(("groups", "tile"), None, None, None),
            P(),
            P(),
            P(("groups", "tile"), None, None, None),
            P(("groups", "tile"), None, None),
            P("groups", None),
        ),
        out_specs=P(("groups", "tile"), None, None, None, None),
        check_vma=False,
    )
```

```python
import functools
import jax
import jax.numpy as jnp
from jax import lax
from jax.experimental import pallas as pl
from jax.experimental.pallas import tpu as pltpu
from jax.sharding import PartitionSpec as P


BLOCK = 128
LANES = 128
SEG = 32


def skew(rows8, base):
    base = base % LANES
    if base > LANES - 8:
        rows8 = pltpu.roll(rows8, 8, 1)
        base -= 8
    return pltpu.roll(rows8, base, 1, stride=1, stride_axis=0)


def iotas(rows):
    lane = lax.broadcasted_iota(jnp.int32, (rows, LANES), 1)
    row = lax.broadcasted_iota(jnp.int32, (rows, LANES), 0)
    return lane, lane - row


def split(x):
    high = x.astype(jnp.bfloat16)
    low = (x - high.astype(jnp.float32)).astype(jnp.bfloat16)
    return high, low


def banded_rows(tap_row, length, taps, first):
    _, diff = iotas(8)
    wide = jnp.broadcast_to(tap_row, (8, LANES))
    tiles = []
    for start in range(0, length, 8):
        rolled = skew(wide, start + first)
        cols = []
        for tile in range(length // LANES):
            k = diff + (LANES * tile - start - first)
            cols.append(jnp.where((k >= 0) & (k < taps), rolled, 0.0))
        tiles.append(jnp.concatenate(cols, axis=1) if len(cols) > 1 else cols[0])
    return jnp.concatenate(tiles, axis=0)


def as_column(row):
    count = row.shape[1]
    lane = lax.broadcasted_iota(jnp.int32, (count, count), 1)
    index = lax.broadcasted_iota(jnp.int32, (count, count), 0)
    return jnp.sum(jnp.where(lane == index, row, 0.0), axis=1, keepdims=True)


def sinc(x):
    angle = jnp.where(x == 0, 1.0, jnp.pi * x)
    return jnp.where(x == 0, 1.0, jnp.sin(angle) / angle)


def fill_matched_coefficients(step, table, h_win, side, filters, taps, length, win):
    half = length // 2
    middle = taps // 2
    origin = side * (length - win)
    lane, diff = iotas(8)
    tiles = -(-filters * SEG // LANES)
    terms = [
        [jnp.broadcast_to(table[6 * t + j, pl.ds(step, 1), :], (8, LANES)) for j in range(6)]
        for t in range(tiles)
    ]
    for group in range(half // 16):
        halves = []
        for sub in range(2):
            start = 16 * group + 8 * sub
            row = lax.broadcasted_iota(jnp.int32, (8, LANES), 0) + (side * half + start)
            u = 2.0 * row.astype(jnp.float32) / (length - 1) - 1.0
            compact = {}
            for tile in range(tiles):
                t = terms[tile]
                compact[0, tile] = t[0] + u * (t[1] + u * t[3])
                compact[1, tile] = t[2] + u * t[4]
                compact[2, tile] = t[5]
            acc = {}
            for b in range(filters):
                lead = b * win + side * half + start - middle - origin
                first = max(lead, b * win)
                last = min(lead + 7 + taps - 1, (b + 1) * win - 1)
                masks = {}
                for tile in range(first // LANES, last // LANES + 1):
                    k = diff + (LANES * tile - lead)
                    mask = (k >= 0) & (k < taps)
                    if lead < b * win:
                        mask &= lane >= b * win - LANES * tile
                    if lead + 7 + taps > (b + 1) * win:
                        mask &= lane < (b + 1) * win - LANES * tile
                    masks[tile] = mask
                source, off = divmod(b * SEG, LANES)
                for q in range(3):
                    rolled = skew(compact[q, source], lead - off)
                    for tile, mask in masks.items():
                        acc[q, tile] = jnp.where(mask, rolled, acc.get((q, tile), 0.0))
            halves.append(acc)
        for q, tile in sorted(set(halves[0]) | set(halves[1])):
            zero = jnp.zeros((8, LANES), jnp.float32)
            both = jnp.concatenate([h.get((q, tile), zero) for h in halves], axis=0)
            h_win[
                side,
                q * half + 16 * group : q * half + 16 * group + 16,
                tile * LANES : (tile + 1) * LANES,
            ] = both.astype(jnp.bfloat16)


def match_kernel(x_ref, c_ref, rtap_ref, ctap_ref, out_ref, pow_ref, *refs, pack, visits):
    rbig, tap_rows, basis, table = refs[:4]
    s_wins = refs[4 : 4 + pack]
    h_wins = refs[4 + pack :]
    filters, taps = rtap_ref.shape
    length = x_ref.shape[1]
    half = length // 2
    middle = taps // 2
    win = -(-(half + middle) // 16) * 16
    step = pl.program_id(0)

    @pl.when(step == 0)
    def _():
        tap_rows[...] = jnp.zeros(tap_rows.shape, jnp.float32)
        tap_rows[0:filters, 0:taps] = rtap_ref[...].astype(jnp.float32)
        tap_rows[8 : 8 + filters, 0:taps] = ctap_ref[...].astype(jnp.float32)
        i = lax.broadcasted_iota(jnp.int32, (LANES, LANES), 0)
        j = lax.broadcasted_iota(jnp.int32, (LANES, LANES), 1)
        flip = (i + j == taps - 1).astype(jnp.float32).astype(jnp.bfloat16)
        flipped = jnp.dot(
            tap_rows[0:8, :].astype(jnp.bfloat16), flip, preferred_element_type=jnp.float32
        )
        for b in range(filters):
            band = banded_rows(flipped[b : b + 1, :], length, taps, -middle)
            rbig[:, b * length : (b + 1) * length] = band.astype(jnp.bfloat16)
        for ref in (*s_wins, *h_wins):
            ref[...] = jnp.zeros(ref.shape, jnp.bfloat16)
        pow_ref[...] = jnp.zeros(pow_ref.shape, jnp.float32)
        basis[...] = jnp.zeros(basis.shape, jnp.float32)
        for a in range(filters):
            row = jnp.broadcast_to(tap_rows[8 + a : 9 + a, :], (8, LANES))
            for b in range(filters):
                tile, off = divmod(b * SEG, LANES)
                moved = pltpu.roll(row, off, 1) if off else row
                basis[a * filters + b : a * filters + b + 1, tile * LANES : (tile + 1) * LANES] = (
                    moved[0:1]
                )
        count, terms = c_ref.shape[1:]
        for tile in range(basis.shape[1] // LANES):
            table[6 * tile : 6 * tile + 6] = jnp.dot(
                c_ref[...].reshape(6 * count, terms),
                basis[0:terms, tile * LANES : (tile + 1) * LANES],
                precision=lax.Precision.HIGHEST,
                preferred_element_type=jnp.float32,
            ).reshape(6, count, LANES)

    col = lax.broadcasted_iota(jnp.int32, (1, length), 1).astype(jnp.float32)
    w = 2.0 * col / (length - 1) - 1.0

    def smooth(n):
        image = x_ref[n].astype(jnp.bfloat16)
        for b in range(filters):
            part = jnp.dot(
                image, rbig[:, b * length : (b + 1) * length], preferred_element_type=jnp.float32
            ).astype(jnp.bfloat16)
            s_wins[n][0, b * win : (b + 1) * win, :] = part[0:win]
            s_wins[n][1, b * win : (b + 1) * win, :] = part[length - win :]

    def fill(n, side):
        fill_matched_coefficients(
            step * pack + n, table, h_wins[n], side, filters, taps, length, win
        )

    def combine(n, side):
        z = jnp.dot(h_wins[n][side], s_wins[n][side], preferred_element_type=jnp.float32)
        matched = z[0:half] + w * (z[half : 2 * half] + w * z[2 * half :])
        out_ref[n, side * half : (side + 1) * half, :] = matched
        squares = jnp.sum(matched * matched, axis=0, keepdims=True)
        visit = pl.ds((step * pack + n) % visits, 1)
        pow_ref[visit, :] = pow_ref[visit, :] + (squares[:, :half] + squares[:, half:])

    smooth(0)
    fill(0, 0)
    for n in range(pack):
        if n + 1 < pack:
            smooth(n + 1)
        fill(n, 1)
        combine(n, 0)
        if n + 1 < pack:
            fill(n + 1, 0)
        combine(n, 1)


def match(images, coeffs, row_taps, col_taps, visits):
    count, length, _ = images.shape
    filters, taps = row_taps.shape
    half = length // 2
    win = -(-(half + taps // 2) // 16) * 16
    depth = -(-filters * win // LANES) * LANES
    pow_rows = -(-visits // 8) * 8
    pack = 2 - count % 2
    tiles = -(-filters * SEG // LANES)
    return pl.pallas_call(
        functools.partial(match_kernel, pack=pack, visits=visits),
        grid=(count // pack,),
        in_specs=[
            pl.BlockSpec((pack, length, length), lambda i: (i, 0, 0)),
            pl.BlockSpec(coeffs.shape, lambda i: (0, 0, 0)),
            pl.BlockSpec(row_taps.shape, lambda i: (0, 0)),
            pl.BlockSpec(col_taps.shape, lambda i: (0, 0)),
        ],
        out_specs=[
            pl.BlockSpec((pack, length, length), lambda i: (i, 0, 0)),
            pl.BlockSpec((pow_rows, LANES), lambda i: (0, 0)),
        ],
        out_shape=[
            jax.ShapeDtypeStruct((count, length, length), jnp.float32),
            jax.ShapeDtypeStruct((pow_rows, LANES), jnp.float32),
        ],
        scratch_shapes=[
            pltpu.VMEM((length, filters * length), jnp.bfloat16),
            pltpu.VMEM((16, LANES), jnp.float32),
            pltpu.VMEM((-(-filters * filters // 8) * 8, tiles * LANES), jnp.float32),
            pltpu.VMEM((6 * tiles, count, LANES), jnp.float32),
        ]
        + [pltpu.VMEM((2, depth, length), jnp.bfloat16)] * pack
        + [pltpu.VMEM((2, 3 * half, depth), jnp.bfloat16)] * pack,
        name="match",
    )(images, coeffs, row_taps, col_taps)


def warp_kernel(own_ref, sub_ref, m_ref, *refs, strips, parts, pack, powers):
    given = refs[:powers]
    outs = refs[powers : powers + strips * parts]
    shifts, held, totals, sems = refs[powers + strips * parts :]
    step = pl.program_id(0)
    half = m_ref.shape[1] // 2
    height = half // strips // parts
    fetches = [
        pltpu.make_async_copy(given[i], totals.at[i], sems.at[i]) for i in range(powers)
    ]

    @pl.when(step == 0)
    def _():
        for fetch in fetches:
            fetch.start()
        lanes = lax.broadcasted_iota(jnp.int32, (1, LANES), 1).astype(jnp.float32)
        for axis, steps in enumerate((2.0 - lanes, lanes - 3.0)):
            distance = steps + as_column(sub_ref[axis : axis + 1, :])
            value = sinc(distance) * sinc(distance / 3.0)
            shifts[axis] = jnp.where(jnp.abs(distance) < 3.0, value, 0.0)

    for n in range(pack):
        image = step * pack + n
        vertical = split(banded_rows(shifts[0, pl.ds(image, 1), :], half, 6, -2))
        horizontal = split(banded_rows(shifts[1, pl.ds(image, 1), :], half, 6, -3))
        left = jnp.concatenate([vertical[0], vertical[0], vertical[1]], axis=1)
        right = jnp.concatenate([horizontal[0], horizontal[0], horizontal[1]], axis=0)
        moved = []
        for side in range(2):
            upper, lower = split(m_ref[n, side * half : (side + 1) * half, :])
            full = jnp.dot(
                left,
                jnp.concatenate([upper, lower, upper], axis=0),
                preferred_element_type=jnp.float32,
            )
            moved += [full[:, :half], full[:, half:]]
        upper, lower = split(jnp.concatenate(moved, axis=0))
        lhs = jnp.concatenate([upper, lower, upper], axis=1)
        held[n] = jnp.dot(lhs, right, preferred_element_type=jnp.float32).reshape(4, half, half)
    for n in range(pack):
        for part in range(parts):
            for k in range(strips):
                begin = (part * strips + (own_ref[0] ^ k)) * height
                rows = pl.ds(pl.multiple_of(begin, height), height)
                for block in range(4):
                    item = 4 * (step * pack + n) + block
                    at = pl.ds(pl.multiple_of(item * height, height), height)
                    outs[part * strips + k][at, :] = held[n, block, rows, :]

    @pl.when(step == pl.num_programs(0) - 1)
    def _():
        for fetch in fetches:
            fetch.wait()
        total = jnp.sum(totals[...], axis=0)
        for out in outs[:strips]:
            out[out.shape[0] - total.shape[0] :, :] = total


def warp(own, subpixel, matched, powers, parts, strips):
    count, length, _ = matched.shape
    half = length // 2
    rows = count * 4 * half // strips // parts
    pow_rows = powers[0].shape[0]
    pack = 2 - count % 2
    shapes = [
        jax.ShapeDtypeStruct((rows + (0 if part else pow_rows), half), jnp.float32)
        for part in range(parts)
        for _ in range(strips)
    ]
    outs = pl.pallas_call(
        functools.partial(
            warp_kernel, strips=strips, parts=parts, pack=pack, powers=len(powers)
        ),
        grid_spec=pltpu.PrefetchScalarGridSpec(
            num_scalar_prefetch=1,
            grid=(count // pack,),
            in_specs=[
                pl.BlockSpec(subpixel.shape, lambda i, own: (0, 0)),
                pl.BlockSpec((pack, length, length), lambda i, own: (i, 0, 0)),
            ]
            + [pl.BlockSpec(memory_space=pltpu.HBM)] * len(powers),
            out_specs=[pl.BlockSpec(x.shape, lambda i, own: (0, 0)) for x in shapes],
            scratch_shapes=[
                pltpu.VMEM((2, count, LANES), jnp.float32),
                pltpu.VMEM((pack, 4, half, half), jnp.float32),
                pltpu.VMEM((len(powers), pow_rows, LANES), jnp.float32),
                pltpu.SemaphoreType.DMA((len(powers),)),
            ],
        ),
        out_shape=shapes,
        name="warp",
    )(own, subpixel, matched, *powers)
    return [outs[part * strips : (part + 1) * strips] for part in range(parts)]


def reduce_kernel(own_ref, dest_ref, slot_ref, *refs, strips, slots, images, visits, pixels):
    pieces = refs[:strips]
    given = refs[strips:-4]
    out_ref, var_ref, acc0, acc1 = refs[-4:]
    pow_rows = var_ref.shape[0]
    height = out_ref.shape[0] // slots
    if given:
        variance = given[0][...]
    else:
        total = pieces[0][pieces[0].shape[0] - pow_rows :, :]
        for piece in pieces[1:]:
            total = total + piece[piece.shape[0] - pow_rows :, :]
        total = jnp.sum(total, axis=1, keepdims=True)
        variance = jnp.broadcast_to(total / pixels + 1e-05, (pow_rows, LANES))
    var_ref[...] = variance
    weight = 1.0 / variance
    acc0[...] = jnp.zeros(acc0.shape, jnp.float32)
    acc1[...] = jnp.zeros(acc1.shape, jnp.float32)
    own = own_ref[0]
    for image in range(images):
        visit = image % visits
        scale = jnp.broadcast_to(weight[visit : visit + 1], (height, LANES))
        for k in range(strips):
            for block in range(4):
                item = 4 * image + block
                acc = acc0 if block % 2 == 0 else acc1
                slot = dest_ref[own ^ k, item]
                at = pl.ds(pl.multiple_of(slot * height, height), height)
                rows = slice(item * height, (item + 1) * height)
                acc[at, :] = acc[at, :] + scale * pieces[k][rows, :]
    devices, items = slot_ref.shape
    lane = lax.broadcasted_iota(jnp.int32, (pow_rows, items), 1)
    row = lax.broadcasted_iota(jnp.int32, (pow_rows, items), 0)
    by_item = jnp.sum(
        jnp.where(lane // 4 % visits == row, weight[:, 0:1], 0.0), axis=0, keepdims=True
    )
    index = lax.broadcasted_iota(jnp.int32, (slots, items), 0)
    hits = jnp.zeros((slots, items), jnp.float32)
    for device in range(devices):
        hits = hits + jnp.where(slot_ref[device : device + 1, :] == index, 1.0, 0.0)
    denom = jnp.sum(hits * by_item, axis=1, keepdims=True)
    inverse = 1.0 / jnp.where(denom > 0, denom, 1.0)
    for slot in range(slots):
        at = slice(slot * height, (slot + 1) * height)
        scale = jnp.broadcast_to(inverse[slot : slot + 1, :], (height, LANES))
        out_ref[at, :] = (acc0[at, :] + acc1[at, :]) * scale


def reduce_blocks(own, dest, pieces, variance, slots, images, visits, pixels):
    pow_rows = -(-visits // 8) * 8
    given = [] if variance is None else [variance]
    height = pieces[0].shape[0] // (images * 4)
    smem = pl.BlockSpec(memory_space=pltpu.SMEM)
    vmem = pl.BlockSpec(memory_space=pltpu.VMEM)
    kernel = functools.partial(
        reduce_kernel,
        strips=len(pieces),
        slots=slots,
        images=images,
        visits=visits,
        pixels=pixels,
    )
    return pl.pallas_call(
        kernel,
        in_specs=[smem, smem] + [vmem] * (1 + len(pieces) + len(given)),
        out_specs=[vmem, vmem],
        out_shape=[
            jax.ShapeDtypeStruct((slots * height, LANES), jnp.float32),
            jax.ShapeDtypeStruct((pow_rows, LANES), jnp.float32),
        ],
        scratch_shapes=[pltpu.VMEM((slots * height, LANES), jnp.float32)] * 2,
        name="reduce_blocks",
    )(own, dest, dest, *pieces, *given)


def finish_kernel(own_ref, dest_ref, var_ref, *refs, groups, visits, aliased):
    count = 2 * len(groups)
    warped = refs[:count]
    templates = refs[count : 2 * count]
    out_ref, held, sems = refs[2 * count + aliased :]
    own = own_ref[0]
    images = out_ref.shape[0]
    height = held.shape[3] // 2
    inverse = 1.0 / jnp.sqrt(var_ref[...])
    copies = []
    for g, (pair, part) in enumerate(groups):
        for image in range(images):
            visit = image % visits
            scale = jnp.broadcast_to(inverse[visit : visit + 1, :], (height, LANES))
            for block in range(4):
                item = 4 * image + block
                at = pl.ds(pl.multiple_of(dest_ref[own, item] * height, height), height)
                for k in range(2):
                    here = warped[2 * g + k][item * height : (item + 1) * height, :]
                    rows = pl.ds(pl.multiple_of(((own & 1) ^ k) * height, height), height)
                    held[g, image, block, rows, :] = (here - templates[2 * g + k][at, :]) * scale
        strip = (own % GROUP // 2) ^ (pair // 2)
        begin = pl.multiple_of((part * GROUP + 2 * strip) * height, 2 * height)
        copies.append(
            pltpu.make_async_copy(
                held.at[g], out_ref.at[:, :, pl.ds(begin, 2 * height), :], sems.at[g]
            )
        )
        copies[-1].start()
    for copy in copies:
        copy.wait()


def finish(own, dest, variance, warped, full, previous, groups, images, visits):
    keys = [(part, k) for pair, part in groups for k in (pair, pair + 1)]
    mine = [warped[part][k] for part, k in keys]
    templates = [full[part][k] for part, k in keys]
    height = BLOCK // GROUP // PARTS
    smem = pl.BlockSpec(memory_space=pltpu.SMEM)
    vmem = pl.BlockSpec(memory_space=pltpu.VMEM)
    hbm = pl.BlockSpec(memory_space=pl.ANY)
    extra = [] if previous is None else [previous]
    inputs = [variance, *mine, *templates]
    return pl.pallas_call(
        functools.partial(finish_kernel, groups=groups, visits=visits, aliased=len(extra)),
        in_specs=[smem, smem] + [vmem] * len(inputs) + [hbm] * len(extra),
        out_specs=hbm,
        out_shape=jax.ShapeDtypeStruct((images, 4, BLOCK, LANES), jnp.float32),
        scratch_shapes=[
            pltpu.VMEM((len(groups), images, 4, 2 * height, LANES), jnp.float32),
            pltpu.SemaphoreType.DMA((len(groups),)),
        ],
        input_output_aliases={2 + len(inputs): 0} if extra else {},
        name="finish",
    )(own, dest, *inputs, *extra)


GROUP = 8
PARTS = 2


def per_device(exposures, row_taps, col_taps, kernel_coeffs, subpixel, destination):
    tile_count, visits, length = exposures.shape[:3]
    filters, _ = row_taps.shape
    devices = lax.axis_size("tile")
    own = lax.axis_index("tile").astype(jnp.int32).reshape(1)
    images = tile_count * visits
    slots = tile_count * devices * 4
    pixels = tile_count * devices * length * length
    dest = destination.reshape(devices, images * 4)

    def permute(x, target):
        return lax.ppermute(x, "tile", [(i, target(i)) for i in range(devices)])

    def swap(x, k):
        return permute(x, lambda i: i ^ k)

    def ahead(x, groups):
        return permute(x, lambda i: (i + groups * GROUP) % devices)

    others = devices // GROUP
    matched, power = match(
        exposures.reshape(images, length, length),
        kernel_coeffs.transpose(3, 0, 1, 2).reshape(-1, images, filters * filters),
        row_taps,
        col_taps,
        visits,
    )
    powers = [power] + [ahead(power, r) for r in range(1, others)]
    shifts = subpixel.transpose(2, 0, 1).reshape(2, images)
    warped = warp(own % GROUP, shifts, matched, powers, PARTS, GROUP)
    pieces = []
    for part in range(PARTS):
        mine = warped[part]
        pieces.append([mine[0]] + [swap(mine[k], k) for k in range(1, GROUP)])
    full = []
    variance = None
    for part in range(PARTS):
        partial, variance = reduce_blocks(
            own, dest, pieces[part], variance, slots, images, visits, pixels
        )
        moved = [ahead(partial, r) for r in range(1, others)]
        template = partial
        for piece in moved:
            template = template + piece
        two = swap(template, 2)
        four = swap(template, 4)
        six = swap(two, 4) if part == 0 else swap(four, 2)
        full.append(
            [template, swap(template, 1)]
            + [two, swap(two, 1)]
            + [four, swap(four, 1)]
            + [six, swap(six, 1)]
        )
    last = GROUP - 2
    early = tuple((pair, part) for part in range(PARTS) for pair in range(0, last, 2))
    late = tuple((last, part) for part in range(PARTS))
    result = None
    for groups in (early, late):
        result = finish(own, dest, variance, warped, full, result, groups, images, visits)
    return result.reshape(tile_count, visits, 4, BLOCK, BLOCK)


def solution(mesh):
    return jax.shard_map(
        per_device,
        mesh=mesh,
        in_specs=(
            P(("groups", "tile"), None, None, None),
            P(),
            P(),
            P(("groups", "tile"), None, None, None),
            P(("groups", "tile"), None, None),
            P("groups", None),
        ),
        out_specs=P(("groups", "tile"), None, None, None, None),
        check_vma=False,
    )
```
